32 devices in a mesh: replica: 8 (over y, x, core), fsdp: 4 (over z).
Axes of the slice: x: 2, y: 2, z: 4, core: 2. Of those that a mesh axis runs over, the one named last changes fastest.
Arguments:
- hidden_in: bfloat16 [9216, 768], P(('replica', 'fsdp')), may hold values from -6 to 6
- segments: int32 [32, 288], P(('replica', 'fsdp')), may hold values from 0 to 18, as said below
- positions: int32 [32, 288], P(('replica', 'fsdp')), may hold values from 0 to 287, as said below
- attn_gain: bfloat16 [768], P('fsdp'), may hold values from 0.25 to 1.75
- attn_shift: bfloat16 [768], P('fsdp'), may hold values from -3 to 3
- mlp_gain: bfloat16 [768], P('fsdp'), may hold values from 0.25 to 1.75
- mlp_shift: bfloat16 [768], P('fsdp'), may hold values from -3 to 3
- w_qkv: bfloat16 [768, 2304], P('fsdp'), may hold values from -0.21875 to 0.21875
- q_bias: bfloat16 [768], P('fsdp'), may hold values from -3 to 3
- v_bias: bfloat16 [768], P('fsdp'), may hold values from -3 to 3
- w_out: bfloat16 [768, 768], P('fsdp'), may hold values from -0.875 to 0.875
- w_up: bfloat16 [768, 3072], P('fsdp'), may hold values from -0.21875 to 0.21875
- up_bias: bfloat16 [3072], P('fsdp'), may hold values from -3 to 3
- w_down: bfloat16 [3072, 768], P('fsdp'), may hold values from -0.109375 to 0.109375
- out_bias: bfloat16 [768], P('fsdp'), may hold values from -3 to 3
- cotangent: bfloat16 [9216, 768], P(('replica', 'fsdp')), may hold values from -6 to 6
Outputs:
- layer_out: bfloat16 [9216, 768], P(('replica', 'fsdp'))
- grad_in: bfloat16 [9216, 768], P(('replica', 'fsdp'))
- grad_attn_gain: float32 [768], P('fsdp')
- grad_attn_shift: float32 [768], P('fsdp')
- grad_mlp_gain: float32 [768], P('fsdp')
- grad_mlp_shift: float32 [768], P('fsdp')
- grad_w_qkv: float32 [768, 2304], P('fsdp')
- grad_q_bias: float32 [768], P('fsdp')
- grad_v_bias: float32 [768], P('fsdp')
- grad_w_out: float32 [768, 768], P('fsdp')
- grad_w_up: float32 [768, 3072], P('fsdp')
- grad_up_bias: float32 [3072], P('fsdp')
- grad_w_down: float32 [3072, 768], P('fsdp')
- grad_out_bias: float32 [768], P('fsdp')
The draws below stay inside these ranges and needn't reach their ends.
Inputs may be any that keep to these rules, and one draw needn't show every extreme that they name: `segments`: along each row the document numbers start at 0 and rise by one at each new document; a token attends to itself and the earlier tokens of its row with the same number; a document that neither begins nor ends its row has 16 or more tokens. `positions`: A token's index within its document.
All inputs are finite; a program needn't handle non-finite values.
Results may differ from the reference program's by a relative error of at most 0.019.
Values may be sent and summed in bfloat16 or wider, within the bound.
No kernel may reach another device: no remote copies, remote signals or barrier semaphores. Data moves between devices by JAX's collectives and lax.ppermute only.
A program may use at most 128 MiB of HBM per device.

```python
import math
import jax
import jax.numpy as jnp
from jax import lax

D = 768
HD = 64
ROT = 16
FF = 3072
SEQ = 288
ROWS = 32
TOKENS = 9216


def document_layout(key):
    folded_key = jax.random.fold_in(key, 7)
    key_gap, key_offset = jax.random.split(folded_key)
    row_index = jnp.arange(ROWS, dtype=jnp.int32)[:, None]
    spacing = jax.random.randint(key_gap, (ROWS, 1), 16, 257).astype(jnp.int32)
    spacing = jnp.where(row_index == 0, 16, jnp.where(row_index == 1, SEQ + 1, spacing)).astype(jnp.int32)
    offset = (jax.random.randint(key_offset, (ROWS, 1), 0, 1048576) % spacing).astype(jnp.int32)
    offset = jnp.where(row_index == 0, 1, jnp.where(row_index == 1, 0, offset)).astype(jnp.int32)
    token_index = jnp.arange(SEQ, dtype=jnp.int32)[None, :]
    cut_flags = (token_index + offset) % spacing == 0
    starts = jnp.logical_or(cut_flags, token_index == 0)
    seg_ids = jnp.cumsum(starts.astype(jnp.int32), axis=1) - 1
    first_token = lax.cummax(jnp.where(starts, token_index, 0), axis=1)
    return (seg_ids.astype(jnp.int32), (token_index - first_token).astype(jnp.int32))


def draw_segments(key, part):
    return document_layout(key)[0]


def draw_positions(key, part):
    return document_layout(key)[1]


def level_of(stream_key, extent, pieces, low, high):
    level, own = 1.0, jax.random.fold_in(stream_key, 6)
    for axis_at, shards_of in pieces:
        heights = jnp.exp(jax.random.uniform(jax.random.fold_in(own, axis_at), (shards_of,), jnp.float32, low / len(pieces), high / len(pieces)))
        level = level * jnp.repeat(heights, extent[axis_at] // shards_of).reshape([-1 if axis == axis_at else 1 for axis in range(len(extent))])
    return level


def scatter_about(rng, shape, spread, limit, cuts=(), kind=jnp.bfloat16):
    drawn = jax.random.normal(rng, shape, jnp.float32) * spread
    if len(cuts) > 0:
        drawn = level_of(rng, shape, cuts, -0.22, 0.18) * drawn
    return jnp.clip(drawn, min=-limit, max=limit).astype(kind)


def setup_inputs(seed: int = 0) -> dict:
    key_list = jax.random.split(jax.random.key(seed), 17)
    hidden_in = scatter_about(key_list[0], (TOKENS, D), 1.0, 6.0, ((0, 32),))
    segments = draw_segments(jax.random.fold_in(key_list[16], 71), 0)
    positions = draw_positions(jax.random.fold_in(key_list[16], 71), 0)
    attn_gain = jnp.clip(1.0 + 0.15 * jax.random.normal(key_list[3], (D,), jnp.float32), 0.25, 1.75).astype(jnp.bfloat16)
    attn_shift = scatter_about(key_list[4], (D,), 0.5, 3.0, ((0, 4),))
    mlp_gain = jnp.clip(1.0 + 0.15 * jax.random.normal(key_list[5], (D,), jnp.float32), 0.25, 1.75).astype(jnp.bfloat16)
    mlp_shift = scatter_about(key_list[6], (D,), 0.5, 3.0, ((0, 4),))
    w_qkv = scatter_about(key_list[7], (D, 3 * D), D ** -0.5, 0.21875, ((0, 4),))
    q_bias = scatter_about(key_list[8], (D,), 0.5, 3.0, ((0, 4),))
    v_bias = scatter_about(key_list[9], (D,), 0.5, 3.0, ((0, 4),))
    w_out = scatter_about(key_list[10], (D, D), (D // 16) ** -0.5, 0.875, ((0, 4),))
    w_up = scatter_about(key_list[11], (D, FF), D ** -0.5, 0.21875, ((0, 4),))
    up_bias = scatter_about(key_list[12], (FF,), 0.5, 3.0, ((0, 4),))
    w_down = scatter_about(key_list[13], (FF, D), FF ** -0.5, 0.109375, ((0, 4),))
    out_bias = scatter_about(key_list[14], (D,), 0.5, 3.0, ((0, 4),))
    cotangent = scatter_about(key_list[15], (TOKENS, D), 1.0, 6.0, ((0, 32),))
    return {"hidden_in": hidden_in, "segments": segments, "positions": positions, "attn_gain": attn_gain, "attn_shift": attn_shift, "mlp_gain": mlp_gain, "mlp_shift": mlp_shift, "w_qkv": w_qkv, "q_bias": q_bias, "v_bias": v_bias, "w_out": w_out, "w_up": w_up, "up_bias": up_bias, "w_down": w_down, "out_bias": out_bias, "cotangent": cotangent}


EPSILON = 1e-05

def normalize(x_f32):
    center = x_f32 - lax.optimization_barrier(jnp.mean(x_f32, axis=-1, keepdims=True))
    inv_dev = lax.rsqrt(lax.optimization_barrier(jnp.mean(center * center, axis=-1, keepdims=True)) + EPSILON)
    return (center * inv_dev, inv_dev)

def angles(positions, rot_dims):
    half_rot = rot_dims // 2
    frequency = jnp.power(10000.0, -jnp.arange(half_rot, dtype=jnp.float32) * (2.0 / rot_dims))
    phase_angle = positions.astype(jnp.float32)[..., None] * frequency
    phase_angle = jnp.concatenate([phase_angle, phase_angle], axis=-1)[:, :, None, :]
    return (jnp.cos(phase_angle), jnp.sin(phase_angle))

def rotate(field_in, cosine, sine):
    rot_dims = cosine.shape[-1]
    half_rot = rot_dims // 2
    rot_part = field_in[..., :rot_dims]
    turned = jnp.concatenate([-rot_part[..., half_rot:], rot_part[..., :half_rot]], axis=-1)
    return jnp.concatenate([rot_part * cosine + turned * sine, field_in[..., rot_dims:]], axis=-1)

def unrotate(grad_field, cosine, sine):
    rot_dims = cosine.shape[-1]
    half_rot = rot_dims // 2
    sined = grad_field[..., :rot_dims] * sine
    turned_back = jnp.concatenate([sined[..., half_rot:], -sined[..., :half_rot]], axis=-1)
    return jnp.concatenate([grad_field[..., :rot_dims] * cosine + turned_back, grad_field[..., rot_dims:]], axis=-1)

def doc_mask(segments):
    seq_len = segments.shape[1]
    token_index = jnp.arange(seq_len, dtype=jnp.int32)
    same_doc = segments[:, :, None] == segments[:, None, :]
    return jnp.logical_and(same_doc, (token_index[:, None] >= token_index[None, :])[None])

def attention_scores(queries, keys_rot, allowed):
    raw_scores = jnp.einsum('rihd,rjhd->rhij', queries.astype(jnp.float32), keys_rot.astype(jnp.float32))
    raw_scores = raw_scores * (1.0 / math.sqrt(HD))
    return jnp.where(allowed[:, None], raw_scores, -jnp.inf)

def forward(hidden_in, segments, positions, attn_gain, attn_shift, mlp_gain, mlp_shift, w_qkv, q_bias, v_bias, w_out, w_up, up_bias, w_down, out_bias):
    num_rows, seq_len = segments.shape
    model_width = hidden_in.shape[1]
    head_shape = (num_rows, seq_len, model_width // HD, HD)
    x_f32 = hidden_in.astype(jnp.float32)
    normed, inv_dev = normalize(x_f32)
    att_in = (normed * attn_gain.astype(jnp.float32) + attn_shift.astype(jnp.float32)).astype(jnp.bfloat16)
    mlp_in = (normed * mlp_gain.astype(jnp.float32) + mlp_shift.astype(jnp.float32)).astype(jnp.bfloat16)
    proj = jnp.dot(att_in, w_qkv, preferred_element_type=jnp.float32)
    cosine, sine = angles(positions, ROT)
    queries = rotate((proj[:, :model_width] + q_bias.astype(jnp.float32)).reshape(head_shape), cosine, sine).astype(jnp.bfloat16)
    keys_rot = rotate(proj[:, model_width:2 * model_width].reshape(head_shape), cosine, sine).astype(jnp.bfloat16)
    values = (proj[:, 2 * model_width:] + v_bias.astype(jnp.float32)).astype(jnp.bfloat16).reshape(head_shape)
    allowed = doc_mask(segments)
    scores = attention_scores(queries, keys_rot, allowed)
    row_top = lax.optimization_barrier(jnp.max(scores, axis=-1, keepdims=True))
    log_total = row_top + jnp.log(lax.optimization_barrier(jnp.sum(jnp.exp(scores - row_top), axis=-1, keepdims=True)))
    attn_probs = jnp.exp(scores - log_total).astype(jnp.bfloat16)
    head_mix = jnp.einsum('rhij,rjhd->rihd', attn_probs.astype(jnp.float32), values.astype(jnp.float32))
    head_mix = head_mix.astype(jnp.bfloat16).reshape(num_rows * seq_len, model_width)
    attn_branch = jnp.dot(head_mix, w_out, preferred_element_type=jnp.float32)
    up_proj = jnp.dot(mlp_in, w_up, preferred_element_type=jnp.float32) + up_bias.astype(jnp.float32)
    activated = jax.nn.gelu(up_proj, approximate=False).astype(jnp.bfloat16)
    mlp_branch = jnp.dot(activated, w_down, preferred_element_type=jnp.float32)
    layer_out = (x_f32 + attn_branch + mlp_branch + out_bias.astype(jnp.float32)).astype(jnp.bfloat16)
    kept_state = (normed, inv_dev, att_in, mlp_in, queries, keys_rot, values, log_total, head_mix, up_proj, activated, cosine, sine, allowed)
    return (layer_out, kept_state)

def backward(kept_state, cotangent, attn_gain, mlp_gain, w_qkv, w_out, w_up, w_down, grad_scale):
    normed, inv_dev, att_in, mlp_in, queries, keys_rot, values, log_total, head_mix, up_proj, activated, cosine, sine, allowed = kept_state
    head_shape = queries.shape
    total_rows, model_width = normed.shape
    cot_f32 = cotangent.astype(jnp.float32)
    grad_out_bias = grad_scale * lax.optimization_barrier(jnp.sum(cot_f32, axis=0))
    grad_w_down = grad_scale * jnp.dot(activated.T, cotangent, preferred_element_type=jnp.float32)
    d_activated = jnp.dot(cotangent, w_down.T, preferred_element_type=jnp.float32)
    normal_cdf = 0.5 * (1.0 + lax.erf(up_proj * (1.0 / math.sqrt(2.0))))
    normal_pdf = jnp.exp(-0.5 * up_proj * up_proj) * (1.0 / math.sqrt(2.0 * math.pi))
    d_upper = d_activated * (normal_cdf + up_proj * normal_pdf)
    grad_up_bias = grad_scale * lax.optimization_barrier(jnp.sum(d_upper, axis=0))
    d_upper16 = d_upper.astype(jnp.bfloat16)
    grad_w_up = grad_scale * jnp.dot(mlp_in.T, d_upper16, preferred_element_type=jnp.float32)
    d_mlp_in = jnp.dot(d_upper16, w_up.T, preferred_element_type=jnp.float32)
    grad_w_out = grad_scale * jnp.dot(head_mix.T, cotangent, preferred_element_type=jnp.float32)
    d_mix = jnp.dot(cotangent, w_out.T, preferred_element_type=jnp.float32).astype(jnp.bfloat16).reshape(head_shape)
    mix_heads = head_mix.reshape(head_shape)
    scores = attention_scores(queries, keys_rot, allowed)
    p_exact = jnp.exp(scores - log_total)
    attn_probs = p_exact.astype(jnp.bfloat16)
    d_values = jnp.einsum('rhij,rihd->rjhd', attn_probs.astype(jnp.float32), d_mix.astype(jnp.float32))
    d_probs = jnp.einsum('rihd,rjhd->rhij', d_mix.astype(jnp.float32), values.astype(jnp.float32))
    row_delta = lax.optimization_barrier(jnp.sum(d_mix.astype(jnp.float32) * mix_heads.astype(jnp.float32), axis=-1))
    row_delta = jnp.transpose(row_delta, (0, 2, 1))[..., None]
    d_scores = (p_exact * (d_probs - row_delta) * (1.0 / math.sqrt(HD))).astype(jnp.bfloat16)
    d_queries = jnp.einsum('rhij,rjhd->rihd', d_scores.astype(jnp.float32), keys_rot.astype(jnp.float32))
    d_keys = jnp.einsum('rhij,rihd->rjhd', d_scores.astype(jnp.float32), queries.astype(jnp.float32))
    d_q = unrotate(d_queries, cosine, sine).reshape(total_rows, model_width)
    d_k = unrotate(d_keys, cosine, sine).reshape(total_rows, model_width)
    d_v = d_values.reshape(total_rows, model_width)
    grad_q_bias = grad_scale * lax.optimization_barrier(jnp.sum(d_q, axis=0))
    grad_v_bias = grad_scale * lax.optimization_barrier(jnp.sum(d_v, axis=0))
    d_proj = jnp.concatenate([d_q, d_k, d_v], axis=1).astype(jnp.bfloat16)
    grad_w_qkv = grad_scale * jnp.dot(att_in.T, d_proj, preferred_element_type=jnp.float32)
    d_att_in = jnp.dot(d_proj, w_qkv.T, preferred_element_type=jnp.float32)
    grad_attn_gain = grad_scale * lax.optimization_barrier(jnp.sum(d_att_in * normed, axis=0))
    grad_attn_shift = grad_scale * lax.optimization_barrier(jnp.sum(d_att_in, axis=0))
    grad_mlp_gain = grad_scale * lax.optimization_barrier(jnp.sum(d_mlp_in * normed, axis=0))
    grad_mlp_shift = grad_scale * lax.optimization_barrier(jnp.sum(d_mlp_in, axis=0))
    d_normed = d_att_in * attn_gain.astype(jnp.float32) + d_mlp_in * mlp_gain.astype(jnp.float32)
    d_center = d_normed - lax.optimization_barrier(jnp.mean(d_normed, axis=-1, keepdims=True)) - normed * lax.optimization_barrier(jnp.mean(d_normed * normed, axis=-1, keepdims=True))
    grad_in = (cot_f32 + inv_dev * d_center).astype(jnp.bfloat16)
    grads = (grad_attn_gain, grad_attn_shift, grad_mlp_gain, grad_mlp_shift, grad_w_qkv, grad_q_bias, grad_v_bias, grad_w_out, grad_w_up, grad_up_bias, grad_w_down, grad_out_bias)
    return (grad_in, grads)

def reference(hidden_in, segments, positions, attn_gain, attn_shift, mlp_gain, mlp_shift, w_qkv, q_bias, v_bias, w_out, w_up, up_bias, w_down, out_bias, cotangent):
    block_rows = math.gcd(ROWS, 16)
    num_blocks = ROWS // block_rows
    grad_scale = 1.0 / math.sqrt(TOKENS)
    weights_all = (attn_gain, attn_shift, mlp_gain, mlp_shift, w_qkv, q_bias, v_bias, w_out, w_up, up_bias, w_down, out_bias)

    def per_block(running, block_args):
        hidden_block, seg_block, pos_block, cot_block = block_args
        layer_block, kept_state = forward(hidden_block, seg_block, pos_block, attn_gain, attn_shift, mlp_gain, mlp_shift, w_qkv, q_bias, v_bias, w_out, w_up, up_bias, w_down, out_bias)
        grad_block, grads = backward(kept_state, cot_block, attn_gain, mlp_gain, w_qkv, w_out, w_up, w_down, grad_scale)
        summed = tuple((left_term + right_term for left_term, right_term in zip(running, grads)))
        return (summed, (layer_block, grad_block))
    initial = tuple((jnp.zeros(weight.shape, jnp.float32) for weight in weights_all))
    block_args = (hidden_in.reshape(num_blocks, block_rows * SEQ, D), segments.reshape(num_blocks, block_rows, SEQ), positions.reshape(num_blocks, block_rows, SEQ), cotangent.reshape(num_blocks, block_rows * SEQ, D))
    grads, (layer_outs, grad_ins) = lax.scan(per_block, initial, block_args)
    return (layer_outs.reshape(TOKENS, D), grad_ins.reshape(TOKENS, D), grads[0], grads[1], grads[2], grads[3], grads[4], grads[5], grads[6], grads[7], grads[8], grads[9], grads[10], grads[11])
```

```python
import math

import jax
import jax.numpy as jnp
from jax import lax
from jax.sharding import PartitionSpec as P

HD = 64
ROT = 16
TP = 4
EPSILON = 1e-05
AXES = ("replica", "fsdp")
BF = jnp.bfloat16
F32 = jnp.float32


class Grid:
    def __init__(self):
        self.replicas = lax.axis_size("replica")
        self.depth = lax.axis_size("fsdp")
        self.outer = self.replicas // (2 * TP)
        replica = lax.axis_index("replica")
        self.core = lax.rem(replica, 2)
        self.tp = lax.rem(replica // 2, TP)
        self.z = lax.axis_index("fsdp")

    def permute(self, x, target):
        pairs = []
        for o in range(self.outer):
            for k in range(TP):
                for c in range(2):
                    for z in range(self.depth):
                        to = target(o, k, c, z)
                        pairs.append((self.flat(o, k, c, z), self.flat(*to)))
        return lax.ppermute(x, AXES, pairs)

    def flat(self, o, k, c, z):
        return ((o * TP + k) * 2 + c) * self.depth + z

    def swap_core(self, x):
        return self.permute(x, lambda o, k, c, z: (o, k, 1 - c, z))

    def swap_tp(self, x, bit):
        return self.permute(x, lambda o, k, c, z: (o, k ^ bit, c, z))

    def shift_z(self, x, s):
        return self.permute(x, lambda o, k, c, z: (o, k, c, (z + s) % self.depth))

    def shift_outer(self, x, s):
        return self.permute(x, lambda o, k, c, z: ((o + s) % self.outer, k, c, z))

    def transpose_tp_z(self, x):
        return self.permute(x, lambda o, k, c, z: (o, z, c, k))


def normalize(x_f32):
    center = x_f32 - jnp.mean(x_f32, axis=-1, keepdims=True)
    inv_dev = lax.rsqrt(jnp.mean(center * center, axis=-1, keepdims=True) + EPSILON)
    return (center * inv_dev, inv_dev)


def angles(positions, rot_dims):
    half_rot = rot_dims // 2
    frequency = jnp.power(10000.0, -jnp.arange(half_rot, dtype=F32) * (2.0 / rot_dims))
    phase_angle = positions.astype(F32)[..., None] * frequency
    phase_angle = jnp.concatenate([phase_angle, phase_angle], axis=-1)[:, :, None, :]
    return (jnp.cos(phase_angle), jnp.sin(phase_angle))


def rotate(field_in, cosine, sine):
    rot_dims = cosine.shape[-1]
    half_rot = rot_dims // 2
    rot_part = field_in[..., :rot_dims]
    turned = jnp.concatenate([-rot_part[..., half_rot:], rot_part[..., :half_rot]], axis=-1)
    return jnp.concatenate([rot_part * cosine + turned * sine, field_in[..., rot_dims:]], axis=-1)


def unrotate(grad_field, cosine, sine):
    rot_dims = cosine.shape[-1]
    half_rot = rot_dims // 2
    sined = grad_field[..., :rot_dims] * sine
    turned_back = jnp.concatenate([sined[..., half_rot:], -sined[..., :half_rot]], axis=-1)
    return jnp.concatenate(
        [grad_field[..., :rot_dims] * cosine + turned_back, grad_field[..., rot_dims:]], axis=-1
    )


def doc_mask(segments):
    seq_len = segments.shape[1]
    token_index = jnp.arange(seq_len, dtype=jnp.int32)
    same_doc = segments[:, :, None] == segments[:, None, :]
    return jnp.logical_and(same_doc, (token_index[:, None] >= token_index[None, :])[None])


def pick(stack, index):
    return lax.dynamic_index_in_dim(stack, index, 0, keepdims=False)


def dot(a, b):
    return jnp.dot(a, b, preferred_element_type=F32)


def dot_tn(a, b):
    return lax.dot_general(a, b, (((0,), (0,)), ((), ())), preferred_element_type=F32)


def dot_nt(a, b):
    return lax.dot_general(a, b, (((1,), (1,)), ((), ())), preferred_element_type=F32)


def plane_gather(g, x, first, second):
    if first == 1:
        near = jnp.concatenate([x, g.swap_tp(x, 1)], axis=0)
        return jnp.concatenate([near, g.swap_tp(near, 2)], axis=0)
    far = g.swap_tp(x, 2)
    both = jnp.stack([x, far])
    other = g.swap_tp(both, 1)
    return jnp.concatenate([x, other[0], far, other[1]], axis=0)


def plane_reduce(g, x, first):
    if first == 1:
        got = g.swap_tp(jnp.stack([x[1], x[3]]).astype(BF), 1)
        own, far = x[0] + got[0].astype(F32), x[2] + got[1].astype(F32)
        return own + g.swap_tp(far.astype(BF), 2).astype(F32)
    got = g.swap_tp(x[2:4].astype(BF), 2)
    own, near = x[0] + got[0].astype(F32), x[1] + got[1].astype(F32)
    return own + g.swap_tp(near.astype(BF), 1).astype(F32)


def local(
    hidden_in,
    segments,
    positions,
    attn_gain,
    attn_shift,
    mlp_gain,
    mlp_shift,
    w_qkv,
    q_bias,
    v_bias,
    w_out,
    w_up,
    up_bias,
    w_down,
    out_bias,
    cotangent,
):
    g = Grid()
    depth = g.depth
    tokens, width = hidden_in.shape
    num_rows, seq_len = segments.shape
    shard = w_qkv.shape[0]
    half = shard // 2
    part = width // TP
    ff_shard = w_down.shape[0]
    ff_part = ff_shard // TP
    ff_half = ff_part // 2
    ff_local = ff_part * depth
    all_tokens = tokens * TP
    heads = part // HD

    marks = jnp.stack(
        [segments.astype(BF), (positions // 16).astype(BF), (positions % 16).astype(BF)], axis=1
    ).reshape(num_rows * 3, seq_len)
    marks_all = plane_gather(g, marks, 1, 2)
    hidden_all = plane_gather(g, hidden_in, 1, 2)
    cot_all = plane_gather(g, cotangent, 2, 1)
    marks_all = marks_all.reshape(TP * num_rows, 3, seq_len)
    seg_all = marks_all[:, 0].astype(jnp.int32)
    pos_all = marks_all[:, 1].astype(jnp.int32) * 16 + marks_all[:, 2].astype(jnp.int32)

    my_qkv = pick(w_qkv.reshape(2, half, 3, TP, part).transpose(0, 3, 1, 2, 4).reshape(2 * TP, half, 3 * part), g.core * TP + g.tp)
    my_up = pick(
        w_up.reshape(2, half, depth, TP, ff_part).transpose(0, 3, 1, 2, 4).reshape(2 * TP, half, ff_local),
        g.core * TP + g.tp,
    )
    my_down = pick(w_down.reshape(TP * 2, ff_half, width), g.tp * 2 + g.core)
    small = jnp.concatenate(
        [attn_gain, attn_shift, mlp_gain, mlp_shift, q_bias, v_bias, out_bias, up_bias]
    )

    def gather_z(x):
        got = [x] + [g.shift_z(x, s) for s in range(1, depth)]
        stack = jnp.stack(got)
        return [pick(stack, lax.rem(g.z - zz + depth, depth)) for zz in range(depth)]

    def with_other_half(pieces):
        mine = jnp.stack(pieces)
        other = g.swap_core(mine)
        lower = jnp.where(g.core == 0, mine, other)
        upper = jnp.where(g.core == 0, other, mine)
        return jnp.stack([lower, upper], axis=1)

    smalls = jnp.stack(gather_z(small))
    wq = with_other_half(gather_z(my_qkv)).reshape(width, 3 * part)
    if depth == TP:
        my_out = pick(w_out.reshape(2, half, width), g.core)
        mine = g.transpose_tp_z(my_out)
        other = g.swap_core(mine)
        wo = jnp.where(
            g.core == 0, jnp.concatenate([mine, other]), jnp.concatenate([other, mine])
        )
    else:
        whole_out = lax.all_gather(w_out, "fsdp", axis=0, tiled=True)
        wo = lax.dynamic_slice_in_dim(whole_out, g.tp * part, part, 0)
    wu = with_other_half(gather_z(my_up)).reshape(width, ff_local)
    wd = with_other_half(gather_z(my_down)).reshape(ff_local, width)

    def vector(i):
        return smalls[:, i * shard : (i + 1) * shard].reshape(width).astype(F32)

    a_gain, a_shift, m_gain, m_shift = vector(0), vector(1), vector(2), vector(3)
    qb = pick(vector(4).reshape(TP, part), g.tp)
    vb = pick(vector(5).reshape(TP, part), g.tp)
    ob = vector(6)
    ub = pick(
        smalls[:, 7 * shard :].reshape(depth, TP, ff_part).transpose(1, 0, 2).reshape(TP, ff_local),
        g.tp,
    ).astype(F32)

    head_shape = (TP * num_rows, seq_len, heads, HD)
    x_f32 = hidden_all.astype(F32)
    normed, inv_dev = normalize(x_f32)
    att_in = (normed * a_gain + a_shift).astype(BF)
    mlp_in = (normed * m_gain + m_shift).astype(BF)
    proj = dot(att_in, wq)
    cosine, sine = angles(pos_all, ROT)
    queries = rotate((proj[:, :part] + qb).reshape(head_shape), cosine, sine).astype(BF)
    keys = rotate(proj[:, part : 2 * part].reshape(head_shape), cosine, sine).astype(BF)
    values = (proj[:, 2 * part :] + vb).astype(BF).reshape(head_shape)
    allowed = doc_mask(seg_all)
    scores = jnp.einsum("rihd,rjhd->rhij", queries, keys, preferred_element_type=F32)
    scores = jnp.where(allowed[:, None], scores * (1.0 / math.sqrt(HD)), -jnp.inf)
    row_top = jnp.max(scores, axis=-1, keepdims=True)
    unscaled = jnp.exp(scores - row_top)
    p_exact = unscaled / jnp.sum(unscaled, axis=-1, keepdims=True)
    attn_probs = p_exact.astype(BF)
    head_mix = jnp.einsum("rhij,rjhd->rihd", attn_probs, values, preferred_element_type=F32)
    mix_heads = head_mix.astype(BF)
    head_mix = mix_heads.reshape(all_tokens, part)
    up_proj = dot(mlp_in, wu) + ub
    normal_cdf = 0.5 * (1.0 + lax.erf(up_proj * (1.0 / math.sqrt(2.0))))
    activated = (up_proj * normal_cdf).astype(BF)
    out_partial = dot(head_mix, wo) + dot(activated, wd)
    branch = plane_reduce(g, out_partial.reshape(TP, tokens, width), 2)
    layer_out = (hidden_in.astype(F32) + branch + ob).astype(BF)

    grad_scale = 1.0 / math.sqrt(tokens * depth * g.replicas)
    g_down = grad_scale * dot_tn(activated, cot_all)
    d_activated = dot_nt(cot_all, wd)
    normal_pdf = jnp.exp(-0.5 * up_proj * up_proj) * (1.0 / math.sqrt(2.0 * math.pi))
    d_upper = d_activated * (normal_cdf + up_proj * normal_pdf)
    g_up_bias = jnp.sum(d_upper, axis=0)
    d_upper16 = d_upper.astype(BF)
    g_up = grad_scale * dot_tn(mlp_in, d_upper16)
    d_mlp_in = dot_nt(d_upper16, wu)

    g_out = grad_scale * dot_tn(head_mix, cot_all)
    d_mix = dot_nt(cot_all, wo).astype(BF).reshape(head_shape)
    d_values = jnp.einsum("rhij,rihd->rjhd", attn_probs, d_mix, preferred_element_type=F32)
    d_probs = jnp.einsum("rihd,rjhd->rhij", d_mix, values, preferred_element_type=F32)
    row_delta = jnp.sum(d_mix.astype(F32) * mix_heads.astype(F32), axis=-1)
    row_delta = jnp.transpose(row_delta, (0, 2, 1))[..., None]
    d_scores = (p_exact * (d_probs - row_delta) * (1.0 / math.sqrt(HD))).astype(BF)
    d_queries = jnp.einsum("rhij,rjhd->rihd", d_scores, keys, preferred_element_type=F32)
    d_keys = jnp.einsum("rhij,rihd->rjhd", d_scores, queries, preferred_element_type=F32)
    d_q = unrotate(d_queries, cosine, sine).reshape(all_tokens, part)
    d_k = unrotate(d_keys, cosine, sine).reshape(all_tokens, part)
    d_v = d_values.reshape(all_tokens, part)
    g_q_bias = jnp.sum(d_q, axis=0)
    g_v_bias = jnp.sum(d_v, axis=0)
    d_proj = jnp.concatenate([d_q, d_k, d_v], axis=1).astype(BF)
    g_qkv = grad_scale * dot_tn(att_in, d_proj)
    d_att_in = dot_nt(d_proj, wq)

    g_a_gain = jnp.sum(d_att_in * normed, axis=0)
    g_a_shift = jnp.sum(d_att_in, axis=0)
    g_m_gain = jnp.sum(d_mlp_in * normed, axis=0)
    g_m_shift = jnp.sum(d_mlp_in, axis=0)
    d_normed = d_att_in * a_gain + d_mlp_in * m_gain
    d_own = plane_reduce(g, d_normed.reshape(TP, tokens, width), 1)
    cot_f32 = cotangent.astype(F32)
    own_normed, own_inv = normalize(hidden_in.astype(F32))
    d_center = (
        d_own
        - jnp.mean(d_own, axis=-1, keepdims=True)
        - own_normed * jnp.mean(d_own * own_normed, axis=-1, keepdims=True)
    )
    grad_in = (cot_f32 + own_inv * d_center).astype(BF)
    g_out_bias = jnp.sum(cot_f32, axis=0)

    def core_sum(x):
        keep = jnp.where(g.core == 0, x[:, 0], x[:, 1])
        give = jnp.where(g.core == 0, x[:, 1], x[:, 0])
        return (keep + g.swap_core(give.astype(BF)).astype(F32)).astype(BF)

    def scatter_z(x):
        total = pick(x, g.z).astype(F32)
        for s in range(1, depth):
            got = g.shift_z(pick(x, lax.rem(g.z + s, depth)), s)
            total = total + got.astype(F32)
        for s in range(1, g.outer):
            pass
        return total

    def outer_sum(x):
        total = x
        for s in range(1, g.outer):
            total = total + g.shift_outer(x.astype(BF), s).astype(F32)
        return total

    def finish(x, first):
        every = plane_gather(g, outer_sum(x).astype(BF)[None], first, 3 - first)
        ordered = jnp.stack([pick(every, jnp.bitwise_xor(g.tp, b)) for b in range(TP)])
        other = g.swap_core(ordered)
        lower = jnp.where(g.core == 0, ordered, other)
        upper = jnp.where(g.core == 0, other, ordered)
        return jnp.stack([lower, upper], axis=1).astype(F32)

    r_down = finish(scatter_z(core_sum(g_down.reshape(depth, 2, ff_half, width))), 1)
    grad_w_down = r_down.reshape(ff_shard, width)
    r_up = finish(scatter_z(core_sum(g_up.reshape(depth, 2, half, ff_local))), 2)
    grad_w_up = r_up.reshape(TP, shard, depth, ff_part).transpose(1, 2, 0, 3).reshape(shard, -1)
    r_qkv = finish(scatter_z(core_sum(g_qkv.reshape(depth, 2, half, 3 * part))), 1)
    grad_w_qkv = r_qkv.reshape(TP, shard, 3, part).transpose(1, 2, 0, 3).reshape(shard, -1)
    if depth == TP:
        quarter = half // depth
        mine = core_sum(g_out.reshape(1, 2, half, width))[0]
        mine = scatter_z(mine.reshape(depth, quarter, width)).astype(BF)
        r_out = finish(g.transpose_tp_z(mine).astype(F32), 2)
        grad_w_out = r_out.transpose(1, 0, 2, 3).reshape(shard, width)
    else:
        full = jnp.zeros((width, width), F32)
        full = lax.dynamic_update_slice_in_dim(full, g_out, g.tp * part, 0).astype(BF)
        share = lax.psum_scatter(full, "fsdp", scatter_dimension=0, tiled=True)
        grad_w_out = lax.psum(share, "replica").astype(F32)

    def whole(v):
        return lax.dynamic_update_slice_in_dim(jnp.zeros((width,), F32), v, g.tp * part, 0)

    spread = jnp.zeros((TP, depth, ff_part), F32)
    spread = lax.dynamic_update_index_in_dim(spread, g_up_bias.reshape(depth, ff_part), g.tp, 0)
    vectors = [g_a_gain, g_a_shift, g_m_gain, g_m_shift, whole(g_q_bias), whole(g_v_bias), g_out_bias]
    vectors = [v.reshape(depth, shard) for v in vectors]
    vectors.append(spread.transpose(1, 0, 2).reshape(depth, ff_shard))
    sums = grad_scale * jnp.concatenate(vectors, axis=1)
    sums = scatter_z((sums + g.swap_core(sums)).astype(BF))
    sums = outer_sum(sums)
    sums = jnp.sum(plane_gather(g, sums.astype(BF)[None], 1, 2).astype(F32), axis=0)

    def share(i):
        return sums[i * shard : (i + 1) * shard]

    return (
        layer_out,
        grad_in,
        share(0),
        share(1),
        share(2),
        share(3),
        grad_w_qkv,
        share(4),
        share(5),
        grad_w_out,
        grad_w_up,
        sums[7 * shard :],
        grad_w_down,
        share(6),
    )


def solution(mesh):
    rows = P(("replica", "fsdp"), None)
    vec = P("fsdp")
    mat = P("fsdp", None)
    return jax.shard_map(
        local,
        mesh=mesh,
        in_specs=(rows, rows, rows, vec, vec, vec, vec, mat, vec, vec, mat, mat, vec, mat, vec, rows),
        out_specs=(rows, rows, vec, vec, vec, vec, mat, vec, vec, mat, mat, vec, mat, vec),
        check_vma=False,
    )
```

```python
import functools
import math

import jax
import jax.numpy as jnp
from jax import lax
from jax.experimental import pallas as pl
from jax.experimental.pallas import tpu as pltpu
from jax.sharding import PartitionSpec as P

HD = 64
ROT = 16
TP = 4
SMALL = 16
EPSILON = 1e-05
AXES = ("replica", "fsdp")
BF = jnp.bfloat16
F32 = jnp.float32
MIB = 1 << 20


class Grid:
    def __init__(self):
        self.replicas = lax.axis_size("replica")
        self.depth = lax.axis_size("fsdp")
        self.outer = self.replicas // (2 * TP)
        replica = lax.axis_index("replica")
        self.core = lax.rem(replica, 2)
        self.tp = lax.rem(replica // 2, TP)
        self.z = lax.axis_index("fsdp")
        self.ids = jnp.stack([self.tp, self.core, self.z]).astype(jnp.int32)

    def permute(self, x, target):
        pairs = []
        for o in range(self.outer):
            for k in range(TP):
                for c in range(2):
                    for z in range(self.depth):
                        to = target(o, k, c, z)
                        pairs.append((self.flat(o, k, c, z), self.flat(*to)))
        return lax.ppermute(x, AXES, pairs)

    def flat(self, o, k, c, z):
        return ((o * TP + k) * 2 + c) * self.depth + z

    def swap_core(self, x):
        return self.permute(x, lambda o, k, c, z: (o, k, 1 - c, z))

    def swap_tp(self, x, bit):
        return self.permute(x, lambda o, k, c, z: (o, k ^ bit, c, z))

    def shift_z(self, x, s):
        return self.permute(x, lambda o, k, c, z: (o, k, c, (z + s) % self.depth))

    def shift_outer(self, x, s):
        return self.permute(x, lambda o, k, c, z: ((o + s) % self.outer, k, c, z))

    def transpose_tp_z(self, x):
        return self.permute(x, lambda o, k, c, z: (o, z, c, k))


def dot(a, b):
    return jnp.dot(a, b, preferred_element_type=F32)


def dot_tn(a, b):
    return lax.dot_general(a, b, (((0,), (0,)), ((), ())), preferred_element_type=F32)


def dot_nt(a, b):
    return lax.dot_general(a, b, (((1,), (1,)), ((), ())), preferred_element_type=F32)


def rows(start, size):
    return pl.ds(pl.multiple_of(start, 16), size)


def normalize(x):
    center = x - jnp.mean(x, axis=-1, keepdims=True)
    inv_dev = lax.rsqrt(jnp.mean(center * center, axis=-1, keepdims=True) + EPSILON)
    return center * inv_dev, inv_dev


def call(kernel, outs, args, name, vmem, scratch=()):
    specs = [pl.BlockSpec(memory_space=pltpu.SMEM)]
    specs += [pl.BlockSpec(memory_space=pltpu.VMEM)] * (len(args) - 1)
    return pl.pallas_call(
        kernel,
        out_shape=[jax.ShapeDtypeStruct(s, d) for s, d in outs],
        in_specs=specs,
        out_specs=[pl.BlockSpec(memory_space=pltpu.VMEM)] * len(outs),
        scratch_shapes=list(scratch),
        compiler_params=pltpu.CompilerParams(vmem_limit_bytes=vmem * MIB),
        name=name,
    )(*args)


def pack_kernel(depth, ids, qkv, up, down, out, *rest):
    vectors, (pa, pm, po) = rest[:8], rest[8:]
    k, c, z = ids[0], ids[1], ids[2]
    shard = qkv.shape[0]
    half = shard // 2
    width = down.shape[1]
    part = width // TP
    ff_shard = down.shape[0]
    ff_part = ff_shard // TP
    ff_half = ff_part // 2
    po[...] = out[rows(c * half, half), :]
    pm[half : half + ff_half, :] = down[rows(k * ff_part + c * ff_half, ff_half), :]
    lane = lax.broadcasted_iota(jnp.int32, (SMALL, width), 1) // shard
    for kk in range(TP):

        @pl.when(k == kk)
        def _(kk=kk):
            q = qkv[rows(c * half, half), :].astype(F32)
            pa[...] = jnp.concatenate(
                [q[:, i * width + kk * part : i * width + (kk + 1) * part] for i in range(3)], axis=1
            ).astype(BF)
            u = up[rows(c * half, half), :].astype(F32)
            pm[0:half, :] = jnp.concatenate(
                [
                    u[:, zz * ff_shard + kk * ff_part : zz * ff_shard + (kk + 1) * ff_part]
                    for zz in range(depth)
                ],
                axis=1,
            ).astype(BF)
            own = [v[...].astype(F32) for v in vectors[:7]]
            own.append(vectors[7][...].astype(F32)[:, kk * ff_part : (kk + 1) * ff_part])
            own.append(jnp.zeros((SMALL - 8, shard), F32))
            block = jnp.concatenate(own, axis=0)
            block = jnp.concatenate([block] * depth, axis=1)
            pm[half + ff_half :, :] = jnp.where(lane == z, block, 0.0).astype(BF)


def mlp_kernel(depth, scale, dims, ids, hn, hf, cn, cf, *rest):
    n, shard, ff_part = dims
    own, other = rest[:depth], rest[depth : 2 * depth]
    part_out, part_norm, keep, give, smalls, vec = rest[2 * depth : 2 * depth + 6]
    wu, wd, xin, act, dup, cot, acc = rest[2 * depth + 6 :]
    c, z = ids[1], ids[2]
    half, ff_half = shard // 2, ff_part // 2
    width = hn.shape[1]
    total = jnp.zeros((SMALL, width), F32)
    for s in range(depth):
        zz = lax.rem(z + depth - s, depth)
        for ref, cc in ((own[s], c), (other[s], 1 - c)):
            wu[rows(zz * shard + cc * half, half), :] = ref[0:half, :]
            wd[rows(zz * ff_part + cc * ff_half, ff_half), :] = ref[half : half + ff_half, :]
        total = total + own[s][half + ff_half :, :].astype(F32)
    smalls[...] = total
    for j in range(TP):
        cot[j * n : (j + 1) * n, :] = (cn if j % 2 == 0 else cf)[(j // 2) * n : (j // 2 + 1) * n, :]
    vec[...] = jnp.zeros_like(vec)
    vec[6:7, :] = scale * jnp.sum(cot[0:n, :].astype(F32), axis=0, keepdims=True)

    def block(h, base, j):
        at = rows((base + j) * n, n)
        normed, _ = normalize(h[rows(j * n, n), :].astype(F32))
        x = (normed * smalls[2:3, :] + smalls[3:4, :]).astype(BF)
        xin[at, :] = x
        up = dot(x, wu[...]) + smalls[7:8, :]
        cdf = 0.5 * (1.0 + lax.erf(up * (1.0 / math.sqrt(2.0))))
        a = (up * cdf).astype(BF)
        act[at, :] = a
        pdf = jnp.exp(-0.5 * up * up) * (1.0 / math.sqrt(2.0 * math.pi))
        d_up = dot_nt(cot[at, :], wd[...]) * (cdf + up * pdf)
        d16 = d_up.astype(BF)
        dup[at, :] = d16
        part_out[at, :] = dot(a, wd[...]).astype(BF)
        d_in = dot_nt(d16, wu[...])
        part_norm[at, :] = (d_in * smalls[2:3, :]).astype(BF)
        vec[2:3, :] += scale * jnp.sum(d_in * normed, axis=0, keepdims=True)
        vec[3:4, :] += scale * jnp.sum(d_in, axis=0, keepdims=True)
        vec[7:8, :] += scale * jnp.sum(d_up, axis=0, keepdims=True)

    for base, h in ((0, hn), (2, hf)):

        @pl.loop(0, 2)
        def _(j, base=base, h=h):
            block(h, base, j)

    def store(size, at):
        for s in range(depth):
            zz = lax.rem(z + s, depth)
            keep[s, at : at + size // 2, :] = acc[rows(zz * size + c * (size // 2), size // 2), :].astype(BF)
            give[s, at : at + size // 2, :] = acc[
                rows(zz * size + (1 - c) * (size // 2), size // 2), :
            ].astype(BF)

    tile = 256
    for left, right, size, at in ((xin, dup, shard, 0), (act, cot, ff_part, half)):

        @pl.loop(0, width // tile)
        def _(t, left=left, right=right):
            cols = pl.ds(pl.multiple_of(t * tile, tile), tile)
            acc[cols, :] = scale * dot_tn(left[:, cols], right[...])

        store(size, at)


def attention_kernel(depth, scale, dims, extra, ids, hn, hf, cn, cf, mn, mf, smalls, vec_in, mo, mnorm, *rest):
    n, shard, part, seq = dims
    own, other = rest[:depth], rest[depth : 2 * depth]
    at = 2 * depth
    wo_refs = rest[at : at + (2 if extra else 1)]
    at += len(wo_refs)
    freq, lanes_in = rest[at : at + 2]
    at += 2
    out_send, out_keep, norm_send, norm_keep, keep, give = rest[at : at + 6]
    at += 6
    if not extra:
        g_out_ref = rest[at]
        at += 1
    wq, wt, wo, xin, cot, mix_all, dproj, acc, vec = rest[at:]
    k, c, z = ids[0], ids[1], ids[2]
    half = shard // 2
    width = hn.shape[1]
    heads = part // HD
    for s in range(depth):
        zz = lax.rem(z + depth - s, depth)
        for ref, cc in ((own[s], c), (other[s], 1 - c)):
            piece = ref[...].astype(F32)
            for i in range(3):
                wq[i, rows(zz * shard + cc * half, half), :] = piece[:, i * part : (i + 1) * part].astype(BF)
    if extra:
        wo[rows(c * half, half), :] = wo_refs[0][...]
        wo[rows((1 - c) * half, half), :] = wo_refs[1][...]
    else:
        wo[...] = wo_refs[0][...]
    for j in range(TP):
        cot[j * n : (j + 1) * n, :] = (cn if j % 2 == 0 else cf)[(j // 2) * n : (j // 2 + 1) * n, :]

    d_row = lax.broadcasted_iota(jnp.int32, (part, part), 0)
    d_col = lax.broadcasted_iota(jnp.int32, (part, part), 1)
    inner = d_col % HD
    turn = jnp.where(
        (inner < ROT // 2) & (d_row == d_col + ROT // 2),
        -1.0,
        jnp.where((inner >= ROT // 2) & (inner < ROT) & (d_row == d_col - ROT // 2), 1.0, 0.0),
    ).astype(BF)
    for i in range(2):
        wt[i] = dot(wq[i], turn).astype(BF)

    def mine(row):
        full = smalls[row : row + 1, :]
        picked = jnp.zeros((1, part), F32)
        for kk in range(TP):
            picked = picked + jnp.where(k == kk, full[:, kk * part : (kk + 1) * part], 0.0)
        return picked

    qb, vb = mine(4), mine(5)
    qb_turned = dot(jnp.broadcast_to(qb, (8, part)).astype(BF), turn)[0:1, :]
    lane = lax.broadcasted_iota(jnp.int32, (1, part), 1)
    spread = lanes_in[...]
    plain = jnp.where(lane % HD < ROT, 0.0, 1.0)
    head_of = [jnp.where(lane // HD == h, 1.0, 0.0).astype(BF) for h in range(heads)]
    r_i = lax.broadcasted_iota(jnp.int32, (seq, seq), 0)
    r_j = lax.broadcasted_iota(jnp.int32, (seq, seq), 1)
    vec[...] = vec_in[...]
    zeros = jnp.zeros((1, part), F32)

    def expand(v):
        hi = v.astype(BF)
        mid = (v - hi.astype(F32)).astype(BF)
        lo = (v - hi.astype(F32) - mid.astype(F32)).astype(BF)
        return dot_tn(jnp.concatenate([hi.astype(F32), mid.astype(F32), lo.astype(F32)], axis=0).astype(BF), spread)

    def block(h_ref, m_ref, base, j, bias):
        gj = base + j
        rows_j = rows(gj * n, n)
        normed, _ = normalize(h_ref[rows(j * n, n), :].astype(F32))
        x = (normed * smalls[0:1, :] + smalls[1:2, :]).astype(BF)
        xin[rows_j, :] = x
        marks = m_ref[j].astype(F32)
        seg = marks[0:1, :]
        phase = freq[...] * (marks[1:2, :] * 16.0 + marks[2:3, :])
        cosine = expand(jnp.cos(phase)) + plain
        sine = expand(jnp.sin(phase))
        seg_i = jnp.sum(jnp.where(r_i == r_j, seg, 0.0), axis=1, keepdims=True)
        allowed = (seg_i == seg) & (r_i >= r_j)
        q = ((dot(x, wq[0]) + qb) * cosine + (dot(x, wt[0]) + qb_turned) * sine).astype(BF)
        key = (dot(x, wq[1]) * cosine + dot(x, wt[1]) * sine).astype(BF)
        val = (dot(x, wq[2]) + vb).astype(BF)
        cj = cot[rows_j, :]
        d_mix = dot_nt(cj, wo[...]).astype(BF)
        mix = jnp.zeros((n, part), F32)
        d_q, d_k, d_v = mix, mix, mix
        for h in range(heads):
            hm = head_of[h]
            q_h, k_h, v_h, dm_h = q * hm, key * hm, val * hm, d_mix * hm
            s = jnp.where(allowed, dot_nt(q_h, key) * (1.0 / math.sqrt(HD)), -jnp.inf)
            e = jnp.exp(s - jnp.max(s, axis=1, keepdims=True))
            p = e * (1.0 / jnp.sum(e, axis=1, keepdims=True))
            p16 = p.astype(BF)
            mix_h = dot(p16, v_h)
            mix = mix + mix_h
            delta = jnp.sum(dm_h.astype(F32) * mix_h.astype(BF).astype(F32), axis=1, keepdims=True)
            ds = (p * (dot_nt(dm_h, val) - delta) * (1.0 / math.sqrt(HD))).astype(BF)
            d_v = d_v + dot_tn(p16, dm_h)
            d_q = d_q + dot(ds, k_h)
            d_k = d_k + dot_tn(ds, q_h)
        mix16 = mix.astype(BF)
        mix_all[rows_j, :] = mix16

        def untwist(g):
            gs = g * sine
            hi = gs.astype(BF)
            lo = (gs - hi.astype(F32)).astype(BF)
            return g * cosine + dot_nt(hi, turn) + dot_nt(lo, turn)

        d_q = untwist(d_q)
        d_k = untwist(d_k)
        dq16, dk16, dv16 = d_q.astype(BF), d_k.astype(BF), d_v.astype(BF)
        dproj[0, rows_j, :] = dq16
        dproj[1, rows_j, :] = dk16
        dproj[2, rows_j, :] = dv16
        d_in = dot_nt(dq16, wq[0]) + dot_nt(dk16, wq[1]) + dot_nt(dv16, wq[2])
        vec[0:1, :] += scale * jnp.sum(d_in * normed, axis=0, keepdims=True)
        vec[1:2, :] += scale * jnp.sum(d_in, axis=0, keepdims=True)
        d_norm = d_in * smalls[0:1, :] + mnorm[rows_j, :].astype(F32)
        out = dot(mix16, wo[...]) + mo[rows_j, :].astype(F32)

        if base == 0:
            out_keep[j] = out
        else:
            out_send[j] = out.astype(BF)

        @pl.when(j == 0)
        def _():
            norm_keep[base // 2] = d_norm

        @pl.when(j == 1)
        def _():
            norm_send[base // 2] = d_norm.astype(BF)

        return bias[0] + jnp.sum(d_q, axis=0, keepdims=True), bias[1] + jnp.sum(d_v, axis=0, keepdims=True)

    bias = (zeros, zeros)
    for base, h_ref, m_ref in ((0, hn, mn), (2, hf, mf)):
        bias = lax.fori_loop(
            0, 2, lambda j, b, base=base, h_ref=h_ref, m_ref=m_ref: block(h_ref, m_ref, base, j, b), bias
        )
    for row, b in ((4, bias[0]), (5, bias[1])):
        for kk in range(TP):

            @pl.when(k == kk)
            def _(row=row, b=b, kk=kk):
                blank = jnp.zeros((1, part), F32)
                vec[row : row + 1, :] = scale * jnp.concatenate(
                    [b if i == kk else blank for i in range(TP)], axis=1
                )

    for i in range(3):
        acc[i] = scale * dot_tn(xin[...], dproj[i])
    g_out = scale * dot_tn(mix_all[...], cot[...])
    if extra:
        wo_acc = mix_all
        wo_acc = None
    else:
        g_out_ref[...] = g_out
    blank = jnp.zeros((half, width - 3 * part), F32)
    for zz in range(depth):
        s = lax.rem(zz + depth - z, depth)
        low = vec[:, zz * shard : (zz + 1) * shard]
        tail = jnp.concatenate([low, jnp.zeros((SMALL, width - shard), F32)], axis=1).astype(BF)
        keep[s, half:, :] = tail
        give[s, half:, :] = tail
        for cc in range(2):
            lo = zz * shard + cc * half
            pieces = [acc[i, lo : lo + half, :] for i in range(3)]
            if extra:
                pieces.append(g_out[cc * half : (cc + 1) * half, zz * part : (zz + 1) * part])
            else:
                pieces.append(blank)
            unit = jnp.concatenate(pieces, axis=1).astype(BF)

            @pl.when(c == cc)
            def _(s=s, unit=unit):
                keep[s, 0:half, :] = unit

            @pl.when(c != cc)
            def _(s=s, unit=unit):
                give[s, 0:half, :] = unit


def unpack_kernel(depth, dims, ids, *rest):
    shard, ff_shard = dims
    pieces, outs = rest[:8], rest[8:]
    o_qkv, o_up, o_down, o_out, o_vec, o_bias = outs
    k, c = ids[0], ids[1]
    half = shard // 2
    ff_part = ff_shard // TP
    ff_half = ff_part // 2
    width = o_down.shape[1]
    part = width // TP
    for kk in range(TP):

        @pl.when(k == kk)
        def _(kk=kk):
            for side in range(2):
                mn, mf, an, af = pieces[4 * side : 4 * side + 4]
                cc = c if side == 0 else 1 - c
                m = [None] * TP
                a = [None] * TP
                for j in range(TP):
                    m[kk ^ j] = (mn if j < 2 else mf)[j % 2]
                    a[kk ^ j] = (an if j % 2 == 0 else af)[j // 2]
                up = [x[0:half, :].astype(F32) for x in m]
                o_up[rows(cc * half, half), :] = jnp.concatenate(
                    [up[b][:, zz * ff_part : (zz + 1) * ff_part] for zz in range(depth) for b in range(TP)],
                    axis=1,
                )
                for b in range(TP):
                    o_down[rows(b * ff_part + cc * ff_half, ff_half), :] = m[b][half : half + ff_half, :].astype(F32)
                att = [x[0:half, :].astype(F32) for x in a]
                o_qkv[rows(cc * half, half), :] = jnp.concatenate(
                    [att[b][:, i * part : (i + 1) * part] for i in range(3) for b in range(TP)], axis=1
                )
                o_out[rows(cc * half, half), :] = jnp.concatenate(
                    [att[b][:, 3 * part : 4 * part] for b in range(TP)], axis=1
                )
                if side == 0:
                    small = [x[half:, 0:shard].astype(F32) for x in a]
                    o_vec[...] = small[0] + small[1] + small[2] + small[3]
                    o_bias[...] = jnp.concatenate([small[b][7:8, 0:ff_part] for b in range(TP)], axis=1)


def local(
    hidden_in,
    segments,
    positions,
    attn_gain,
    attn_shift,
    mlp_gain,
    mlp_shift,
    w_qkv,
    q_bias,
    v_bias,
    w_out,
    w_up,
    up_bias,
    w_down,
    out_bias,
    cotangent,
):
    g = Grid()
    depth = g.depth
    tokens, width = hidden_in.shape
    num_rows, seq = segments.shape
    shard = w_qkv.shape[0]
    half = shard // 2
    part = width // TP
    ff_shard = w_down.shape[0]
    ff_part = ff_shard // TP
    ff_half = ff_part // 2
    ff_local = ff_part * depth
    whole = TP * tokens
    square = depth == TP
    grad_scale = 1.0 / math.sqrt(tokens * depth * g.replicas)

    h1 = g.swap_tp(hidden_in, 1)
    c2 = g.swap_tp(cotangent, 2)
    vectors = [attn_gain, attn_shift, mlp_gain, mlp_shift, q_bias, v_bias, out_bias, up_bias]
    pa, pm, po = call(
        functools.partial(pack_kernel, depth),
        [((half, 3 * part), BF), ((half + ff_half + SMALL, width), BF), ((half, width), BF)],
        [g.ids, w_qkv, w_up, w_down, w_out] + [v.reshape(1, -1) for v in vectors],
        "pack",
        24,
    )
    pms = [pm] + [g.shift_z(pm, s) for s in range(1, depth)]
    pas = [pa] + [g.shift_z(pa, s) for s in range(1, depth)]
    marks = jnp.stack(
        [segments.astype(BF), (positions // 16).astype(BF), (positions % 16).astype(BF)], axis=1
    )
    mn = jnp.concatenate([marks, g.swap_tp(marks, 1)], axis=0)
    hn = jnp.concatenate([hidden_in, h1], axis=0)
    cn = jnp.concatenate([cotangent, c2], axis=0)
    hf = g.swap_tp(hn, 2)
    cf = g.swap_tp(cn, 1)
    mf = g.swap_tp(mn, 2)
    pms_other = [g.swap_core(x) for x in pms]
    pas_other = [g.swap_core(x) for x in pas]
    if square:
        wo_own = g.transpose_tp_z(po)
        wo_parts = [wo_own, g.swap_core(wo_own)]
    else:
        all_out = lax.all_gather(w_out, "fsdp", axis=0, tiled=True)
        wo_parts = [lax.dynamic_slice_in_dim(all_out, g.tp * part, part, 0)]

    unit_m = half + ff_half
    unit_a = half + SMALL
    mo, mnorm, m_keep, m_give, smalls, vec = call(
        functools.partial(mlp_kernel, depth, grad_scale, (tokens, shard, ff_part)),
        [
            ((whole, width), BF),
            ((whole, width), BF),
            ((depth, unit_m, width), BF),
            ((depth, unit_m, width), BF),
            ((SMALL, width), F32),
            ((SMALL, width), F32),
        ],
        [g.ids, hn, hf, cn, cf] + pms + pms_other,
        "mlp",
        56,
        [
            pltpu.VMEM((width, ff_local), BF),
            pltpu.VMEM((ff_local, width), BF),
            pltpu.VMEM((whole, width), BF),
            pltpu.VMEM((whole, ff_local), BF),
            pltpu.VMEM((whole, ff_local), BF),
            pltpu.VMEM((whole, width), BF),
            pltpu.VMEM((width, width), F32),
        ],
    )

    def scatter(keep, give):
        summed = keep.astype(F32) + g.swap_core(give).astype(F32)
        sent = summed.astype(BF)
        total = summed[0]
        for s in range(1, depth):
            total = total + g.shift_z(sent[s], s).astype(F32)
        if g.outer > 1:
            mine = total
            for s in range(1, g.outer):
                total = total + g.shift_outer(mine.astype(BF), s).astype(F32)
        return total.astype(BF)

    fm = scatter(m_keep, m_give)

    frequency = jnp.power(10000.0, -jnp.arange(ROT // 2, dtype=F32) * (2.0 / ROT)).reshape(ROT // 2, 1)
    lane = jnp.arange(part)[None, :]
    spread = ((lane % HD < ROT) & (lane % HD % (ROT // 2) == jnp.arange(3 * (ROT // 2))[:, None] % (ROT // 2))).astype(BF)
    attn_outs = [
        ((2, tokens, width), BF),
        ((2, tokens, width), F32),
        ((2, tokens, width), BF),
        ((2, tokens, width), F32),
        ((depth, unit_a, width), BF),
        ((depth, unit_a, width), BF),
    ]
    if not square:
        attn_outs.append(((part, width), F32))
    got = call(
        functools.partial(attention_kernel, depth, grad_scale, (tokens, shard, part, seq), square),
        attn_outs,
        [g.ids, hn, hf, cn, cf, mn, mf, smalls, vec, mo, mnorm] + pas + pas_other + wo_parts + [frequency, spread],
        "attention",
        56,
        [
            pltpu.VMEM((3, width, part), BF),
            pltpu.VMEM((2, width, part), BF),
            pltpu.VMEM((part, width), BF),
            pltpu.VMEM((whole, width), BF),
            pltpu.VMEM((whole, width), BF),
            pltpu.VMEM((whole, part), BF),
            pltpu.VMEM((3, whole, part), BF),
            pltpu.VMEM((3, width, part), F32),
            pltpu.VMEM((SMALL, width), F32),
        ],
    )
    out_send, out_keep, norm_send, norm_keep, a_keep, a_give = got[:6]

    far = g.swap_tp(out_send, 2)
    near = g.swap_tp((out_keep[1] + far[1].astype(F32)).astype(BF), 1)
    branch = out_keep[0] + far[0].astype(F32) + near.astype(F32)
    layer_out = (hidden_in.astype(F32) + branch + smalls[6:7, :]).astype(BF)
    far = g.swap_tp(norm_send, 1)
    near = g.swap_tp((norm_keep[1] + far[1].astype(F32)).astype(BF), 2)
    d_own = norm_keep[0] + far[0].astype(F32) + near.astype(F32)
    own_normed, own_inv = normalize(hidden_in.astype(F32))
    d_center = (
        d_own
        - jnp.mean(d_own, axis=-1, keepdims=True)
        - own_normed * jnp.mean(d_own * own_normed, axis=-1, keepdims=True)
    )
    grad_in = (cotangent.astype(F32) + own_inv * d_center).astype(BF)

    fa = scatter(a_keep, a_give)
    if square:
        turned = g.transpose_tp_z(fa[:half, 3 * part :])
        fa = jnp.concatenate(
            [fa[:, : 3 * part], jnp.concatenate([turned, fa[half:, 3 * part :]], axis=0)], axis=1
        )
    fmn = jnp.stack([fm, g.swap_tp(fm, 1)])
    fmf = g.swap_tp(fmn, 2)
    fan = jnp.stack([fa, g.swap_tp(fa, 2)])
    faf = g.swap_tp(fan, 1)
    pieces = [fmn, fmf, fan, faf]
    pieces += [g.swap_core(x) for x in pieces]
    g_qkv, g_up, g_down, g_out, vecs, g_bias = call(
        functools.partial(unpack_kernel, depth, (shard, ff_shard)),
        [
            ((shard, 3 * width), F32),
            ((shard, ff_part * TP * depth), F32),
            ((ff_shard, width), F32),
            ((shard, width), F32),
            ((SMALL, shard), F32),
            ((1, ff_shard), F32),
        ],
        [g.ids] + pieces,
        "unpack",
        40,
    )
    if not square:
        full = jnp.zeros((width, width), F32)
        full = lax.dynamic_update_slice_in_dim(full, got[6], g.tp * part, 0).astype(BF)
        share = lax.psum_scatter(full, "fsdp", scatter_dimension=0, tiled=True)
        g_out = lax.psum(share, "replica").astype(F32)
    return (
        layer_out,
        grad_in,
        vecs[0],
        vecs[1],
        vecs[2],
        vecs[3],
        g_qkv,
        vecs[4],
        vecs[5],
        g_out,
        g_up,
        g_bias.reshape(-1),
        g_down,
        vecs[6],
    )


def solution(mesh):
    rows_spec = P(("replica", "fsdp"), None)
    vec = P("fsdp")
    mat = P("fsdp", None)
    return jax.shard_map(
        local,
        mesh=mesh,
        in_specs=(rows_spec,) * 3 + (vec,) * 4 + (mat, vec, vec, mat, mat, vec, mat, vec, rows_spec),
        out_specs=(rows_spec, rows_spec, vec, vec, vec, vec, mat, vec, vec, mat, mat, vec, mat, vec),
        check_vma=False,
    )
```
